128 devices in a mesh: refl: 4 (over y_hi, core), atom: 32 (over z, x, y_lo).
Axes of the slice: x: 4, y: 4 (y_hi: 2, y_lo: 2; y = y_hi * 2 + y_lo), z: 4, core: 2. Of those that a mesh axis runs over, the one named last changes fastest.
Arguments:
- features: bfloat16 [65536, 128], P('atom'), may hold values from -6 to 6
- ln_gain: float32 [2, 128], replicated, may hold values from 0.25 to 1.75
- w_qkv: bfloat16 [2, 3, 128, 128], P(None, None, None, 'refl'), may hold values from -0.5 to 0.5
- w_out: bfloat16 [2, 128, 128], replicated, may hold values from -0.5 to 0.5
- w_coord: bfloat16 [3, 128], replicated, may hold values from -0.5 to 0.5
- noisy_coords: float32 [3, 65536], P(None, 'atom'), may hold values from 0 to 1
- scatter_power: float32 [65536], P('atom'), may hold values from 0.5 to 4
- route: int32 [32, 32], P('atom'), may hold values from 0 to 31, each once within a row
- miller: int32 [3, 4096], P(None, 'refl'), may hold values from -12 to 12
- rotations: int32 [4, 3, 3], replicated, may hold values from -1 to 1, as said below
- shifts: float32 [4, 3], replicated, may hold values from 0 to 1
- observed: float32 [4096], P('refl'), may hold values from 0.3 to 3
- obs_weight: float32 [4096], P('refl'), may hold values from 0.2 to 2
Outputs:
- atom_out: bfloat16 [65536, 128], P('atom')
- amplitude: float32 [4096], P(('refl', 'atom'))
- coord_grad: float32 [3, 65536], P(None, 'atom')
The draws below stay inside these ranges and needn't reach their ends.
Inputs may be any that keep to these rules, and one draw needn't show every extreme that they name: Each row of route names every block of a shard once. `rotations`: each of the 4 matrices is a permutation matrix with signs.
All inputs are finite; a program needn't handle non-finite values.
Results may differ from the reference program's by a relative error of at most 0.012.
Values may be sent and summed in bfloat16 or wider, within the bound.
No kernel may reach another device: no remote copies, remote signals or barrier semaphores. Data moves between devices by JAX's collectives and lax.ppermute only.
A program may use at most 64 MiB of HBM per device.

```python
import math
import jax
import jax.numpy as jnp
from jax import lax

C = 128
HEAD_FEATURES = 32
QWIN = 32
WINDOW_KEYS = 128
LAYERS = 2
NOPS = 4
ATOM_DEV = 2048
NATOM = 65536
NREFL = 4096
SLOTS = 32


def draw_rotations(key, part):
    keys = jax.random.split(jax.random.fold_in(key, 71), NOPS)
    perms = jnp.stack([jax.random.permutation(keys[s], 3) for s in range(NOPS)])
    signs = jax.random.randint(jax.random.fold_in(key, 72), (NOPS, 3), 0, 2) * 2 - 1
    columns = jnp.arange(3, dtype=jnp.int32)
    onehot = (perms[:, :, None] == columns[None, None, :]).astype(jnp.int32)
    return (onehot * signs[:, :, None]).astype(jnp.int32)


def plant(entries, own_key, least, top_value):
    spot = [jax.random.randint(jax.random.fold_in(own_key, axis), (), 0, length) for axis, length in enumerate(entries.shape)]
    longest = entries.shape.index(max(entries.shape))
    neighbour = spot[:longest] + [(spot[longest] + 1) % entries.shape[longest]] + spot[longest + 1:]
    return entries.at[tuple(spot)].set(least).at[tuple(neighbour)].set(top_value)


def level_of(key, dims, cuts, least, largest):
    factor_of = 1.0
    for axis_at, blocks in cuts:
        steps = jax.random.uniform(jax.random.fold_in(jax.random.fold_in(key, 6), axis_at), (blocks,), jnp.float32, least / len(cuts), largest / len(cuts))
        factor_of = factor_of * jnp.repeat(jnp.exp(steps), dims[axis_at] // blocks).reshape((-1,) + (1,) * (len(dims) - 1 - axis_at))
    return factor_of


def bell_draw(key, dims, width, limit, cuts=(), held_as=jnp.bfloat16):
    entries = jax.random.normal(key, dims, jnp.float32) * width
    if len(cuts) > 0:
        entries = level_of(key, dims, cuts, -0.22, 0.18) * entries
    return jnp.clip(entries, min=-limit, max=limit).astype(held_as)


def setup_inputs(seed: int = 0) -> dict:
    key_list = jax.random.split(jax.random.key(seed), 14)
    return {
        "features": bell_draw(key_list[0], (NATOM, C), 1.0, 6.0, ((0, 32),)),
        "ln_gain": jnp.clip(1.0 + 0.15 * jax.random.normal(key_list[1], (LAYERS, C), jnp.float32), 0.25, 1.75),
        "w_qkv": bell_draw(key_list[2], (LAYERS, 3, C, C), C ** -0.5, 0.5, ((3, 4),)),
        "w_out": bell_draw(key_list[3], (LAYERS, C, C), C ** -0.5, 0.5),
        "w_coord": bell_draw(key_list[4], (3, C), C ** -0.5, 0.5),
        "noisy_coords": jnp.clip(1.0 * jax.random.uniform(key_list[5], (3, NATOM), jnp.float32) ** level_of(key_list[5], (3, NATOM), ((1, 32),), -0.2, 0.2), 0.0, 1.0),
        "scatter_power": jnp.clip(jnp.exp(math.log(4.0) - 2.0794415 * jax.random.uniform(key_list[6], (NATOM,), jnp.float32) ** level_of(key_list[6], (NATOM,), ((0, 32),), -0.2, 0.2)), 0.5, 4.0),
        "route": jax.vmap(lambda own: jax.random.permutation(own, SLOTS))(jax.random.split(key_list[7], SLOTS)).reshape((SLOTS, SLOTS)).astype(jnp.int32),
        "miller": plant(jax.random.randint(key_list[8], (3, NREFL), -12, 13), jax.random.fold_in(key_list[8], 1), -12, 12).astype(jnp.int32),
        "rotations": draw_rotations(jax.random.fold_in(key_list[13], 71), 0),
        "shifts": jnp.clip(jax.random.uniform(key_list[10], (NOPS, 3), jnp.float32, 0.0, 1.0), 0.0, 1.0),
        "observed": jnp.clip(jnp.exp(math.log(3.0) - 2.3025851 * jax.random.uniform(key_list[11], (NREFL,), jnp.float32) ** level_of(key_list[11], (NREFL,), ((0, 4),), -0.2, 0.2)), 0.3, 3.0),
        "obs_weight": jnp.clip(jnp.exp(math.log(2.0) - 2.3025851 * jax.random.uniform(key_list[12], (NREFL,), jnp.float32) ** level_of(key_list[12], (NREFL,), ((0, 4),), -0.2, 0.2)), 0.2, 2.0),
    }


def layer_norm(x, gain):
    mean = lax.optimization_barrier(jnp.mean(x, axis=-1, keepdims=True))
    cent = x - mean
    var = lax.optimization_barrier(jnp.mean(cent * cent, axis=-1, keepdims=True))
    return (cent * lax.rsqrt(var + 1e-05) * gain).astype(jnp.bfloat16)

def window_blocks(padded, window_count):
    parts = [padded[QWIN * j:QWIN * j + window_count * QWIN].reshape(window_count, QWIN, -1) for j in range(WINDOW_KEYS // QWIN)]
    return jnp.concatenate(parts, axis=1)

def attend_windowed(query_rows, padded_keys, padded_values, valid_mask):
    window_count = query_rows.shape[0] // QWIN
    head_count = query_rows.shape[1] // HEAD_FEATURES
    qwin = query_rows.reshape(window_count, QWIN, head_count, HEAD_FEATURES).astype(jnp.float32)
    kwin = window_blocks(padded_keys, window_count).reshape(window_count, WINDOW_KEYS, head_count, HEAD_FEATURES).astype(jnp.float32)
    window_values = window_blocks(padded_values, window_count).reshape(window_count, WINDOW_KEYS, head_count, HEAD_FEATURES).astype(jnp.float32)
    mwin = window_blocks(valid_mask, window_count)[..., 0]
    scores = jnp.einsum('wqhd,wkhd->whqk', qwin, kwin) * HEAD_FEATURES ** (-0.5)
    scores = jnp.where(mwin[:, None, None, :] > 0.5, scores, -1e+30)
    top = lax.optimization_barrier(jnp.max(scores, axis=-1, keepdims=True))
    expo = jnp.exp(scores - top)
    probs = (expo / lax.optimization_barrier(jnp.sum(expo, axis=-1, keepdims=True))).astype(jnp.bfloat16)
    out = jnp.einsum('whqk,wkhd->wqhd', probs.astype(jnp.float32), window_values)
    return out.reshape(window_count * QWIN, head_count * HEAD_FEATURES).astype(jnp.bfloat16)

def phases(hs_blk, tsh_blk, pos):
    turn = hs_blk[:, 0, :, None] * pos[0] + hs_blk[:, 1, :, None] * pos[1] + hs_blk[:, 2, :, None] * pos[2]
    angle = 2.0 * math.pi * (turn + tsh_blk[:, :, None])
    return (jnp.cos(angle), jnp.sin(angle))

def reference(features, ln_gain, w_qkv, w_out, w_coord, noisy_coords, scatter_power, route, miller, rotations, shifts, observed, obs_weight):
    window_border = (WINDOW_KEYS - QWIN) // 2
    x = features.astype(jnp.float32)
    place = jnp.arange(NATOM + 2 * window_border, dtype=jnp.int32) - window_border
    valid_mask = ((place >= 0) & (place < NATOM)).astype(jnp.float32)[:, None]
    for layer in range(LAYERS):
        normed = layer_norm(x, ln_gain[layer])
        query_rows = jnp.dot(normed, w_qkv[layer, 0], preferred_element_type=jnp.float32).astype(jnp.bfloat16)
        keys = jnp.dot(normed, w_qkv[layer, 1], preferred_element_type=jnp.float32).astype(jnp.bfloat16)
        value_rows = jnp.dot(normed, w_qkv[layer, 2], preferred_element_type=jnp.float32).astype(jnp.bfloat16)
        padded_keys = jnp.pad(keys, ((window_border, window_border), (0, 0)))
        padded_values = jnp.pad(value_rows, ((window_border, window_border), (0, 0)))
        head_rows = attend_windowed(query_rows, padded_keys, padded_values, valid_mask)
        x = x + jnp.dot(head_rows, w_out[layer], preferred_element_type=jnp.float32)
    atom_out = x.astype(jnp.bfloat16)
    moved = noisy_coords + 0.02 * jnp.dot(w_coord, atom_out.T, preferred_element_type=jnp.float32)
    blk = ATOM_DEV // SLOTS
    source = jnp.arange(SLOTS, dtype=jnp.int32)
    index = source[None, :, None] * ATOM_DEV + route.T.astype(jnp.int32)[:, :, None] * blk + jnp.arange(blk, dtype=jnp.int32)[None, None, :]
    index = index.reshape(-1)
    pos = moved[:, index]
    power = scatter_power[index]
    hs = jnp.einsum('skc,kr->scr', rotations.astype(jnp.float32), miller.astype(jnp.float32), precision=lax.Precision.HIGHEST)
    tsh = jnp.einsum('kr,sk->sr', miller.astype(jnp.float32), shifts, precision=lax.Precision.HIGHEST)
    norm = 1.0 / math.sqrt(NOPS * NATOM)
    rows = min(128, NREFL)
    turns = NREFL // rows
    hs_b = hs.reshape(NOPS, 3, turns, rows).transpose(2, 0, 1, 3)
    ts_b = tsh.reshape(NOPS, turns, rows).transpose(1, 0, 2)

    def forward(item):
        cosv, sinv = phases(item[0], item[1], pos)
        fa = jnp.einsum('sra,a->r', cosv, power, precision=lax.Precision.HIGHEST)
        fb = jnp.einsum('sra,a->r', sinv, power, precision=lax.Precision.HIGHEST)
        return jnp.stack([fa, fb]) * norm
    parts = lax.map(forward, (hs_b, ts_b))
    totals = parts.transpose(1, 0, 2).reshape(2, NREFL)
    amplitude = jnp.sqrt(totals[0] * totals[0] + totals[1] * totals[1] + 1.0)
    slope = 2.0 * obs_weight * (amplitude - observed) / (amplitude * math.sqrt(NREFL))
    slopes = jnp.stack([slope * totals[0], slope * totals[1]])
    sl_b = slopes.reshape(2, turns, rows).transpose(1, 0, 2)

    def backward(total, item):
        cosv, sinv = phases(item[0], item[1], pos)
        coef = 2.0 * math.pi * norm * power * (cosv * item[2][1][None, :, None] - sinv * item[2][0][None, :, None])
        return (total + jnp.einsum('scr,sra->ca', item[0], coef, precision=lax.Precision.HIGHEST), None)
    coord_grad, unused = lax.scan(backward, jnp.zeros((3, NATOM), jnp.float32), (hs_b, ts_b, sl_b))
    return (atom_out, amplitude, coord_grad)
```

```python
import functools
import math

import jax
import jax.numpy as jnp
from jax import lax
from jax.experimental import pallas as pl
from jax.experimental.pallas import tpu as pltpu
from jax.sharding import PartitionSpec as P

HEAD = 32
QWIN = 32
KWIN = 128
BORDER = (KWIN - QWIN) // 2
LAYERS = 2
HALO = 128
TOP = 12
ROWS = 640
BF = jnp.bfloat16
F32 = jnp.float32
LANES = (((1,), (1,)), ((), ()))


def dot(a, b, dims=(((1,), (0,)), ((), ()))):
    return lax.dot_general(a, b, dims, preferred_element_type=F32)


def cos_turns(t):
    t = t - jnp.round(t)
    s = 0.25 - jnp.abs(t)
    z = s * s
    p = 81.6010046 + z * (39.5368083 * z - 76.5497956)
    return s * (6.28318516 + z * (z * p - 41.341655))


def full_terms(x):
    i = lax.broadcasted_iota(jnp.int32, (32, 1), 0)
    sine = i > TOP
    freq = jnp.where(sine, i - TOP, i).astype(F32)
    shift = jnp.where(sine, 0.25, 0.0).astype(F32)
    live = jnp.where(i <= 2 * TOP, 1.0, 0.0).astype(F32)
    return cos_turns(freq * x - shift) * live


def part_terms(x):
    i = lax.broadcasted_iota(jnp.int32, (2 * TOP, 1), 0)
    sine = i >= TOP
    freq = jnp.where(sine, i - TOP + 1, i + 1).astype(F32)
    shift = jnp.where(sine, 0.25, 0.0).astype(F32)
    return cos_turns(freq * x - shift)


def fill_products(p_ref, v, w):
    for j in range(TOP):
        a = v[2 * j : 2 * j + 1] * w
        b = v[2 * j + 1 : 2 * j + 2] * w
        p_ref[48 * j : 48 * j + 48, :] = jnp.concatenate([a, b], axis=0).astype(BF)
    last = v[24:25] * w
    pad = jnp.zeros((8, v.shape[1]), F32)
    p_ref[576:640, :] = jnp.concatenate([last, v, pad], axis=0).astype(BF)


def picks(m, rows, first):
    i = lax.broadcasted_iota(jnp.int32, (rows, m.shape[1]), 0) + first
    size = jnp.abs(m)
    sign = jnp.clip(m, -1, 1).astype(F32)
    return (
        jnp.where(i == size, 1.0, 0.0).astype(F32),
        jnp.where(i == size + TOP, sign, 0.0).astype(F32),
    )


def fill_picks(re_ref, im_ref, k, l):
    ck, sk = picks(k, 32, 0)
    cl, sl = picks(l, 2 * TOP, 1)
    flat = jnp.where(l == 0, 1.0, 0.0).astype(F32)

    def real(j):
        return ck[j : j + 1] * cl - sk[j : j + 1] * sl

    def imag(j):
        return ck[j : j + 1] * sl + sk[j : j + 1] * cl

    pad = jnp.zeros((8, k.shape[1]), F32)
    for ref, own, tail in ((re_ref, real, ck * flat), (im_ref, imag, sk * flat)):
        for j in range(TOP):
            pair = jnp.concatenate([own(2 * j), own(2 * j + 1)], axis=0)
            ref[48 * j : 48 * j + 48, :] = pair.astype(BF)
        ref[576:640, :] = jnp.concatenate([own(24), tail, pad], axis=0).astype(BF)


def split(a, count):
    parts = []
    for _ in range(count):
        hi = a.astype(BF)
        parts.append(hi)
        a = a - hi.astype(F32)
    return jnp.concatenate(parts, axis=0)


def images(pos, rot_ref, shf_ref, s):
    rows = []
    for k in range(3):
        r = shf_ref[s, k] + rot_ref[s, 3 * k].astype(F32) * pos[0:1]
        r = r + rot_ref[s, 3 * k + 1].astype(F32) * pos[1:2]
        rows.append(r + rot_ref[s, 3 * k + 2].astype(F32) * pos[2:3])
    return rows


def attend_kernel(
    natom,
    norm,
    nops,
    span,
    rank_ref,
    route_ref,
    rot_ref,
    shf_ref,
    prev_ref,
    feat_ref,
    next_ref,
    wqkv_ref,
    wout_ref,
    gain_ref,
    wcoord_ref,
    noisy_ref,
    power_ref,
    miller_ref,
    out_ref,
    pay_ref,
    x_ref,
    q_ref,
    k_ref,
    v_ref,
    pos_ref,
    p_ref,
    g_ref,
    re_ref,
    im_ref,
    f_ref,
):
    local = feat_ref.shape[0]
    x_ref[0:HALO, :] = prev_ref[...].astype(F32)
    x_ref[HALO : HALO + local, :] = feat_ref[...].astype(F32)
    x_ref[HALO + local :, :] = next_ref[...].astype(F32)
    origin = rank_ref[0] * local - HALO
    head_of = lax.broadcasted_iota(jnp.int32, (QWIN, 128), 1) // HEAD
    lane = lax.broadcasted_iota(jnp.int32, (1, KWIN), 1)
    scale = HEAD**-0.5 * math.log2(math.e)

    for layer in range(LAYERS):
        edge = 64 * layer
        weights = jnp.concatenate(
            [wqkv_ref[g, layer, j] for j in range(3) for g in range(4)], axis=0
        )
        gain = gain_ref[layer : layer + 1, :]

        def project(i, _):
            r = pl.multiple_of(edge + i * 128, 64)
            xc = x_ref[pl.ds(r, 128), :]
            cent = xc - jnp.mean(xc, axis=1, keepdims=True)
            var = jnp.mean(cent * cent, axis=1, keepdims=True)
            normed = (cent * lax.rsqrt(var + 1e-05) * gain).astype(BF)
            proj = dot(normed, weights, LANES).astype(BF)
            q_ref[pl.ds(r, 128), :] = proj[:, 0:128]
            k_ref[pl.ds(r, 128), :] = proj[:, 128:256]
            v_ref[pl.ds(r, 128), :] = proj[:, 256:384]
            return 0

        lax.fori_loop(0, (local + 2 * HALO) // 128 - layer, project, 0)
        w_out = wout_ref[layer]
        first = 64 * (layer + 1)

        def attend(i, _):
            base = pl.multiple_of(first + i * 128, 64)
            heads = []
            for win in range(4):
                r = base + win * QWIN
                qw = q_ref[pl.ds(pl.multiple_of(r, 32), QWIN), :]
                at = pl.multiple_of(r - BORDER, 16)
                kw = k_ref[pl.ds(at, KWIN), :]
                vw = v_ref[pl.ds(at, KWIN), :]
                qm = jnp.concatenate(
                    [jnp.where(head_of == h, qw, jnp.zeros_like(qw)) for h in range(4)], axis=0
                )
                s = dot(qm, kw, LANES)
                place = lane + (origin + at)
                s = jnp.where((place >= 0) & (place < natom), s, -1e30)
                e = jnp.exp2((s - jnp.max(s, axis=1, keepdims=True)) * scale)
                probs = (e / jnp.sum(e, axis=1, keepdims=True)).astype(BF)
                o = dot(probs, vw)
                own = jnp.zeros((QWIN, 128), F32)
                for h in range(4):
                    own = jnp.where(head_of == h, o[QWIN * h : QWIN * h + QWIN], own)
                heads.append(own.astype(BF))
            y = dot(jnp.concatenate(heads, axis=0), w_out)
            x_ref[pl.ds(base, 128), :] += y
            return 0

        lax.fori_loop(0, local // 128 + 1 - layer, attend, 0)

    pos_ref[...] = jnp.zeros_like(pos_ref)
    pos_ref[3:4, :] = power_ref[...]
    step = 256
    for i in range(local // step):
        at = slice(i * step, (i + 1) * step)
        done = x_ref[HALO + i * step : HALO + (i + 1) * step, :].astype(BF)
        out_ref[at, :] = done
        pos_ref[0:3, at] = noisy_ref[:, at] + 0.02 * dot(wcoord_ref[...], done, LANES)

    g_ref[...] = jnp.zeros_like(g_ref)
    chunks = local // span

    def sums(i, _):
        s = i // chunks
        at = pl.multiple_of((i % chunks) * span, span)
        pos = pos_ref[:, pl.ds(at, span)]
        x0, x1, x2 = images(pos, rot_ref, shf_ref, s)
        u = split(full_terms(x0) * pos[3:4], 2)
        fill_products(p_ref, full_terms(x1), part_terms(x2))
        g_ref[...] += dot(u, p_ref[...], LANES)
        return 0

    lax.fori_loop(0, nops * chunks, sums, 0)
    grid = split(g_ref[0:32, :] + g_ref[32:64, :], 3)
    group = miller_ref.shape[1]
    wide = re_ref.shape[1]
    for c in range(group // wide):
        m = miller_ref[:, c * wide : (c + 1) * wide]
        fill_picks(re_ref, im_ref, m[1:2], m[2:3])
        yr = dot(grid, re_ref[...])
        yi = dot(grid, im_ref[...])
        yr = yr[0:32] + yr[32:64] + yr[64:96]
        yi = yi[0:32] + yi[32:64] + yi[64:96]
        uc, us = picks(m[0:1], 32, 0)
        fa = jnp.sum(uc * yr - us * yi, axis=0, keepdims=True) * norm
        fb = jnp.sum(uc * yi + us * yr, axis=0, keepdims=True) * norm
        for b in range(wide // 128):
            row = c * (wide // 128) + b
            f_ref[row : row + 1, :] = fa[:, b * 128 : (b + 1) * 128]
            f_ref[row + 8 : row + 9, :] = fb[:, b * 128 : (b + 1) * 128]

    both = f_ref[...]
    for e in range(pay_ref.shape[0]):
        blk = route_ref[0, e]
        at = pl.multiple_of((blk // 2) * 128, 128)
        piece = pos_ref[:, pl.ds(at, 128)]
        odd = jnp.full(piece.shape, blk % 2, jnp.int32) == 1
        pay_ref[e, 0:16, :] = both
        pay_ref[e, 16:24, :] = jnp.where(odd, pltpu.roll(piece, 64, 1), piece)


def gradient_kernel(
    nrefl,
    norm,
    nops,
    span,
    rot_ref,
    shf_ref,
    recv_ref,
    miller_ref,
    obs_ref,
    wt_ref,
    amp_ref,
    grad_ref,
    pos_ref,
    p_ref,
    w_ref,
    re_ref,
    im_ref,
):
    shards = recv_ref.shape[0]
    total = recv_ref[0, 0:16, :]
    for e in range(1, shards):
        total = total + recv_ref[e, 0:16, :]
    fa, fb = total[0:8], total[8:16]
    amp = jnp.sqrt(fa * fa + fb * fb + 1.0)
    slope = 2.0 * wt_ref[...] * (amp - obs_ref[...]) / (amp * math.sqrt(nrefl))
    amp_ref[...] = amp
    ga, gb = slope * fa, slope * fb
    left = lax.broadcasted_iota(jnp.int32, (8, 128), 1) < 64
    for j in range(shards // 2):
        other = pltpu.roll(recv_ref[2 * j + 1, 16:24, :], 64, 1)
        pos_ref[:, 128 * j : 128 * j + 128] = jnp.where(left, recv_ref[2 * j, 16:24, :], other)

    group = miller_ref.shape[1]
    wide = re_ref.shape[1]
    rows = wide // 128
    for c in range(group // wide):
        m = miller_ref[:, c * wide : (c + 1) * wide]
        fill_picks(re_ref, im_ref, m[1:2], m[2:3])
        uc, us = picks(m[0:1], 32, 0)
        a = jnp.concatenate([ga[c * rows + b : c * rows + b + 1] for b in range(rows)], axis=1)
        b = jnp.concatenate([gb[c * rows + b : c * rows + b + 1] for b in range(rows)], axis=1)
        real = b * uc - a * us
        imag = -(a * uc + b * us)
        mf = m.astype(F32)
        real = split(jnp.concatenate([mf[k : k + 1] * real for k in range(3)], axis=0), 2)
        imag = split(jnp.concatenate([mf[k : k + 1] * imag for k in range(3)], axis=0), 2)
        part = dot(real, re_ref[...], LANES) + dot(imag, im_ref[...], LANES)
        part = part[0:96] + part[96:192]
        w_ref[...] = part if c == 0 else w_ref[...] + part
    coef = split(w_ref[...], 2)
    local = pos_ref.shape[1]
    grad_ref[...] = jnp.zeros_like(grad_ref)
    chunks = local // span
    factor = 2.0 * math.pi * norm

    def slopes(i, _):
        s = i // chunks
        at = pl.multiple_of((i % chunks) * span, span)
        pos = pos_ref[:, pl.ds(at, span)]
        x0, x1, x2 = images(pos, rot_ref, shf_ref, s)
        u = full_terms(x0)
        fill_products(p_ref, full_terms(x1), part_terms(x2))
        t = dot(coef, p_ref[...])
        t = t[0:96] + t[96:192]
        scale = pos[3:4] * factor
        g = [jnp.sum(u * t[32 * k : 32 * k + 32], axis=0, keepdims=True) * scale for k in range(3)]
        for c in range(3):
            r = rot_ref[s, c].astype(F32) * g[0]
            r = r + rot_ref[s, 3 + c].astype(F32) * g[1]
            r = r + rot_ref[s, 6 + c].astype(F32) * g[2]
            grad_ref[c : c + 1, pl.ds(at, span)] += r
        return 0

    lax.fori_loop(0, nops * chunks, slopes, 0)


def body(
    features,
    ln_gain,
    w_qkv,
    w_out,
    w_coord,
    noisy_coords,
    scatter_power,
    route,
    miller,
    rotations,
    shifts,
    observed,
    obs_weight,
):
    shards = lax.axis_size("atom")
    rank = lax.axis_index("atom")
    local = features.shape[0]
    natom = local * shards
    group = miller.shape[1]
    nops = rotations.shape[0]
    nrefl = group * lax.axis_size("refl")
    norm = 1.0 / math.sqrt(nops * natom)
    span = 512
    wide = 256
    smem = pl.BlockSpec(memory_space=pltpu.SMEM)
    vmem = pl.BlockSpec(memory_space=pltpu.VMEM)

    ends = shards - 1
    before = lax.ppermute(features[local - HALO :], "atom", [(i, i + 1) for i in range(ends)])
    after = lax.ppermute(features[:HALO], "atom", [(i + 1, i) for i in range(ends)])
    weights = lax.all_gather(w_qkv.transpose(0, 1, 3, 2), "refl")
    rot = rotations.reshape(nops, 9)
    params = pltpu.CompilerParams(vmem_limit_bytes=60 * 1024 * 1024)
    atom_out, payload = pl.pallas_call(
        functools.partial(attend_kernel, natom, norm, nops, span),
        out_shape=(
            jax.ShapeDtypeStruct((local, 128), BF),
            jax.ShapeDtypeStruct((shards, 24, 128), F32),
        ),
        in_specs=[smem] * 4 + [vmem] * 10,
        out_specs=(vmem, vmem),
        scratch_shapes=[
            pltpu.VMEM((local + 2 * HALO, 128), F32),
            pltpu.VMEM((local + 2 * HALO, 128), BF),
            pltpu.VMEM((local + 2 * HALO, 128), BF),
            pltpu.VMEM((local + 2 * HALO, 128), BF),
            pltpu.VMEM((8, local), F32),
            pltpu.VMEM((ROWS, span), BF),
            pltpu.VMEM((64, ROWS), F32),
            pltpu.VMEM((ROWS, wide), BF),
            pltpu.VMEM((ROWS, wide), BF),
            pltpu.VMEM((16, 128), F32),
        ],
        compiler_params=params,
        name="attend",
    )(
        rank.reshape(1),
        route,
        rot,
        shifts,
        before,
        features,
        after,
        weights,
        w_out,
        ln_gain,
        w_coord,
        noisy_coords,
        scatter_power[None, :],
        miller,
    )
    recv = lax.all_to_all(payload, "atom", split_axis=0, concat_axis=0, tiled=True)
    amp, grad = pl.pallas_call(
        functools.partial(gradient_kernel, nrefl, norm, nops, span),
        out_shape=(
            jax.ShapeDtypeStruct((8, 128), F32),
            jax.ShapeDtypeStruct((3, local), F32),
        ),
        in_specs=[smem] * 2 + [vmem] * 4,
        out_specs=(vmem, vmem),
        scratch_shapes=[
            pltpu.VMEM((8, local), F32),
            pltpu.VMEM((ROWS, span), BF),
            pltpu.VMEM((96, ROWS), F32),
            pltpu.VMEM((ROWS, wide), BF),
            pltpu.VMEM((ROWS, wide), BF),
        ],
        compiler_params=params,
        name="gradient",
    )(rot, shifts, recv, miller, observed.reshape(8, 128), obs_weight.reshape(8, 128))
    grad = grad + lax.ppermute(grad, "refl", [(0, 1), (1, 0), (2, 3), (3, 2)])
    grad = grad + lax.ppermute(grad, "refl", [(0, 2), (2, 0), (1, 3), (3, 1)])
    share = group // shards
    amplitude = lax.dynamic_slice_in_dim(amp.reshape(group), rank * share, share, 0)
    return (atom_out, amplitude, grad)


def solution(mesh):
    placed = (
        P("atom", None),
        P(),
        P(None, None, None, "refl"),
        P(),
        P(),
        P(None, "atom"),
        P("atom"),
        P("atom", None),
        P(None, "refl"),
        P(),
        P(),
        P("refl"),
        P("refl"),
    )
    return jax.shard_map(
        body,
        mesh=mesh,
        in_specs=placed,
        out_specs=(P("atom", None), P(("refl", "atom")), P(None, "atom")),
        check_vma=False,
    )
```

```python
import functools
import math

import jax
import jax.numpy as jnp
from jax import lax
from jax.experimental import pallas as pl
from jax.experimental.pallas import tpu as pltpu
from jax.sharding import PartitionSpec as P

HEAD = 32
QWIN = 32
KWIN = 128
BORDER = (KWIN - QWIN) // 2
LAYERS = 2
HALO = 128
SPAN = 1024
TABLE_SPAN = 512
TOP = 12
ROWS = 640
BF = jnp.bfloat16
F32 = jnp.float32
LANES = (((1,), (1,)), ((), ()))


def dot(a, b, dims=(((1,), (0,)), ((), ()))):
    return lax.dot_general(a, b, dims, preferred_element_type=F32)


def cos_turns(t):
    t = t - jnp.round(t)
    s = 0.25 - jnp.abs(t)
    z = s * s
    p = 81.6010046 + z * (39.5368083 * z - 76.5497956)
    return s * (6.28318516 + z * (z * p - 41.341655))


COSINES = TOP + 1
ORDER = list(range(COSINES)) + list(range(17, 17 + TOP))


def part_rows(i):
    sine = i >= TOP
    freq = jnp.where(i >= 16, i - 15, jnp.where(sine, i - 3, i))
    return freq.astype(F32), sine


def prepare(pos_ref, tab_ref, span):
    row = lax.broadcasted_iota(jnp.int32, (8, span), 0)
    bits = [(row & (1 << b)) != 0 for b in range(3)]
    low = row < 4

    def fill(i, _):
        at = pl.multiple_of(i * span, span)
        x = pos_ref[:, pl.ds(at, span)]
        cos_x, sin_x = cos_turns(x), cos_turns(x - 0.25)
        for k in range(3):
            c1 = jnp.broadcast_to(cos_x[k : k + 1], row.shape)
            s1 = jnp.broadcast_to(sin_x[k : k + 1], row.shape)
            c2, s2 = 1.0 - 2.0 * (s1 * s1), 2.0 * (s1 * c1)
            c4, s4 = 1.0 - 2.0 * (s2 * s2), 2.0 * (s2 * c2)
            c8, s8 = 1.0 - 2.0 * (s4 * s4), 2.0 * (s4 * c4)
            c, s = jnp.where(bits[0], c1, 1.0), jnp.where(bits[0], s1, 0.0)
            for bit, cm, sm in ((bits[1], c2, s2), (bits[2], c4, s4)):
                c, s = jnp.where(bit, c * cm - s * sm, c), jnp.where(bit, s * cm + c * sm, s)
            cb, sb = c * c8 - s * s8, s * c8 + c * s8
            cn, sn = c * c1 - s * s1, s * c1 + c * s1
            ct, st = cn * c8 - sn * s8, sn * c8 + cn * s8
            mid = jnp.where(low, cb, pltpu.roll(st, 4, 0))
            mid_other = jnp.where(low, sb, pltpu.roll(ct, 4, 0))
            for r, part in enumerate((c, cb, s, sb, c, mid, sn, s, mid_other, cn)):
                tab_ref[k, 8 * r : 8 * r + 8, pl.ds(at, span)] = part
        return 0

    lax.fori_loop(0, pos_ref.shape[1] // span, fill, 0)


def rotors(rot_ref, shf_ref, rotor_ref):
    lane = lax.broadcasted_iota(jnp.int32, (1, 128), 1)
    turn = jnp.zeros((1, 128), F32)
    sign = jnp.ones((1, 128), F32)
    nops = rotor_ref.shape[0]
    for s in range(nops):
        for k in range(3):
            here = lane == 3 * s + k
            whole = rot_ref[s, k, 0] + rot_ref[s, k, 1] + rot_ref[s, k, 2]
            turn = jnp.where(here, shf_ref[s, k], turn)
            sign = jnp.where(here, whole.astype(F32), sign)
    i = lax.broadcasted_iota(jnp.int32, (32, 1), 0)
    tables = [((i % 16).astype(F32), i >= 16)] * 2
    tables.append(part_rows(lax.broadcasted_iota(jnp.int32, (24, 1), 0)))
    for k, (freq, sine) in enumerate(tables):
        angle = freq * turn
        same = cos_turns(angle) * jnp.where(sine, sign, 1.0)
        other = cos_turns(angle - 0.25) * jnp.where(sine, 1.0, -sign)
        size = freq.shape[0]
        for s in range(nops):
            j = 3 * s + k
            spread = (size, 128)
            rotor_ref[s, 0, 32 * k : 32 * k + size, :] = jnp.broadcast_to(same[:, j : j + 1], spread)
            rotor_ref[s, 1, 32 * k : 32 * k + size, :] = jnp.broadcast_to(other[:, j : j + 1], spread)
    freq = jnp.full((8, 1), float(TOP), F32)
    same, other = cos_turns(freq * turn), cos_turns(freq * turn - 0.25) * -sign
    for s in range(nops):
        j = 3 * s + 2
        rotor_ref[s, 0, 88:96, :] = jnp.broadcast_to(same[:, j : j + 1], (8, 128))
        rotor_ref[s, 1, 88:96, :] = jnp.broadcast_to(other[:, j : j + 1], (8, 128))


def images(rot_ref, tab_ref, rotor_ref, v_ref, p_ref, s, at, span):
    def table(k, r, size):
        axis = jnp.abs(rot_ref[s, k, 1]) + 2 * jnp.abs(rot_ref[s, k, 2])
        return tab_ref[axis, r : r + size, pl.ds(at, span)]

    def factor(kind, r, size):
        return jnp.concatenate([rotor_ref[s, kind, r : r + size, :]] * (span // 128), axis=1)

    def both(k):
        c, n = table(k, 0, 16), table(k, 16, 16)
        cos = factor(0, 32 * k, 16) * c + factor(1, 32 * k, 16) * n
        sin = factor(0, 32 * k + 16, 16) * n + factor(1, 32 * k + 16, 16) * c
        return jnp.concatenate([cos, sin], axis=0)

    v = both(1)
    v_ref[...] = v
    w = factor(0, 64, 24) * table(2, 32, 24) + factor(1, 64, 24) * table(2, 56, 24)
    c12 = table(2, 8, 8)[4:5]
    s12 = table(2, 24, 8)[4:5]
    last = factor(0, 88, 8)[0:1] * c12 + factor(1, 88, 8)[0:1] * s12

    def row(j):
        return v_ref[ORDER[j] : ORDER[j] + 1, :]

    for j in range(TOP):
        pair = jnp.concatenate([row(2 * j) * w, row(2 * j + 1) * w], axis=0)
        p_ref[48 * j : 48 * j + 48, :] = pair.astype(BF)
    pad = jnp.zeros((8, span), F32)
    p_ref[576:640, :] = jnp.concatenate([row(24) * w, v * last, pad], axis=0).astype(BF)
    return both(0)


def picks(m):
    i = lax.broadcasted_iota(jnp.int32, (32, m.shape[1]), 0)
    size = jnp.abs(m)
    sign = jnp.clip(m, -1, 1).astype(F32)
    return (
        jnp.where(i == size, 1.0, 0.0).astype(F32),
        jnp.where(i == size + 16, sign, 0.0).astype(F32),
    )


def fill_picks(re_ref, im_ref, k, l):
    ck, sk = picks(k)
    i = lax.broadcasted_iota(jnp.int32, (24, l.shape[1]), 0)
    size = jnp.abs(l)
    sign = jnp.clip(l, -1, 1).astype(F32)
    cl = jnp.where(i == jnp.where(size < TOP, size, -1), 1.0, 0.0).astype(F32)
    sl = jnp.where(i == jnp.where(size >= 9, size + 3, size + 15), sign, 0.0).astype(F32)
    top = jnp.where(size == TOP, 1.0, 0.0).astype(F32)

    def real(j):
        r = ORDER[j]
        return ck[r : r + 1] * cl if r < 16 else -sk[r : r + 1] * sl

    def imag(j):
        r = ORDER[j]
        return ck[r : r + 1] * sl if r < 16 else sk[r : r + 1] * cl

    pad = jnp.zeros((8, k.shape[1]), F32)
    for ref, own, tail in ((re_ref, real, ck * top), (im_ref, imag, sk * top)):
        for j in range(TOP):
            pair = jnp.concatenate([own(2 * j), own(2 * j + 1)], axis=0)
            ref[48 * j : 48 * j + 48, :] = pair.astype(BF)
        ref[576:640, :] = jnp.concatenate([own(24), tail, pad], axis=0).astype(BF)


def split(a, count):
    parts = []
    for _ in range(count):
        hi = a.astype(BF)
        parts.append(hi)
        a = a - hi.astype(F32)
    return jnp.concatenate(parts, axis=0)


def attend_kernel(
    natom,
    nops,
    span,
    rot_ref,
    shf_ref,
    feat_ref,
    halo_ref,
    wqkv_ref,
    wout_ref,
    gain_ref,
    wcoord_ref,
    noisy_ref,
    power_ref,
    out_ref,
    half_ref,
    part_ref,
    x_ref,
    x1_ref,
    q_ref,
    k_ref,
    v_ref,
    pos_ref,
    tab_ref,
    rotor_ref,
    t_ref,
    p_ref,
    g_ref,
):
    mine = half_ref.shape[0]
    core = lax.axis_index("refl") % 2
    start = pl.multiple_of(core * mine, mine)
    rotors(rot_ref, shf_ref, rotor_ref)
    first_half = jnp.full((HALO, 128), core, jnp.int32) == 0
    halo = halo_ref[...].astype(F32)
    left = feat_ref[mine - HALO : mine, :].astype(F32)
    right = feat_ref[mine : mine + HALO, :].astype(F32)
    x_ref[0:HALO, :] = jnp.where(first_half, halo, left)
    x_ref[HALO : HALO + mine, :] = feat_ref[pl.ds(start, mine), :].astype(F32)
    x_ref[HALO + mine :, :] = jnp.where(first_half, right, halo)
    origin = lax.axis_index("atom") * feat_ref.shape[0] + start - HALO
    head_of = lax.broadcasted_iota(jnp.int32, (QWIN, 128), 1) // HEAD
    lane = lax.broadcasted_iota(jnp.int32, (1, KWIN), 1)
    scale = HEAD**-0.5 * math.log2(math.e)

    for layer in range(LAYERS):
        edge = 64 * layer
        size = x_ref.shape[0]
        part = min(size // 2, 640)
        from_ref, dest_ref = (x_ref, x1_ref) if layer == 0 else (x1_ref, x_ref)
        weights = jnp.concatenate(
            [wqkv_ref[g, layer, j] for j in range(3) for g in range(4)], axis=0
        )
        gain = gain_ref[layer : layer + 1, :]

        def project(i, _):
            r = pl.multiple_of(jnp.minimum(edge + i * part, size - edge - part), 64)
            xc = from_ref[pl.ds(r, part), :]
            cent = xc - jnp.mean(xc, axis=1, keepdims=True)
            var = jnp.mean(cent * cent, axis=1, keepdims=True)
            normed = (cent * lax.rsqrt(var + 1e-05) * gain).astype(BF)
            proj = dot(normed, weights, LANES).astype(BF)
            q_ref[pl.ds(r, part), :] = proj[:, 0:128]
            k_ref[pl.ds(r, part), :] = proj[:, 128:256]
            v_ref[pl.ds(r, part), :] = proj[:, 256:384]
            return 0

        lax.fori_loop(0, -(-(size - 2 * edge) // part), project, 0)
        w_out = wout_ref[layer]
        first = 64 * (layer + 1)
        rows = mine + 128 * (1 - layer)
        block = 64 * -(-rows // 128)
        ones = jnp.ones((KWIN, 128), BF)

        def attend(i, _):
            base = pl.multiple_of(jnp.minimum(first + i * block, first + rows - block), 64)
            scores = []
            for win in range(block // QWIN):
                r = base + win * QWIN
                qw = q_ref[pl.ds(pl.multiple_of(r, 32), QWIN), :]
                at = pl.multiple_of(r - BORDER, 16)
                kw = k_ref[pl.ds(at, KWIN), :]
                qm = jnp.concatenate(
                    [jnp.where(head_of == h, qw, jnp.zeros_like(qw)) for h in range(4)], axis=0
                )
                s = dot(qm, kw, LANES)
                place = lane + (origin + at)
                scores.append(jnp.where((place >= 0) & (place < natom), s, -1e30))
            tops = [jnp.max(s, axis=1, keepdims=True) for s in scores]
            heads = []
            for win in range(block // QWIN):
                at = pl.multiple_of(base + win * QWIN - BORDER, 16)
                vw = v_ref[pl.ds(at, KWIN), :]
                e = jnp.exp2((scores[win] - tops[win]) * scale).astype(BF)
                o = dot(e, jnp.concatenate([vw, ones], axis=1))
                o = o[:, 0:128] / o[:, 128:256]
                own = jnp.zeros((QWIN, 128), F32)
                for h in range(4):
                    own = jnp.where(head_of == h, o[QWIN * h : QWIN * h + QWIN], own)
                heads.append(own.astype(BF))
            y = dot(jnp.concatenate(heads, axis=0), w_out)
            dest_ref[pl.ds(base, block), :] = from_ref[pl.ds(base, block), :] + y
            return 0

        lax.fori_loop(0, -(-rows // block), attend, 0)

    pos_ref[...] = jnp.zeros_like(pos_ref)
    pos_ref[3:4, :] = power_ref[:, pl.ds(start, mine)]
    step = 256
    for i in range(mine // step):
        at = slice(i * step, (i + 1) * step)
        done = x_ref[HALO + i * step : HALO + (i + 1) * step, :].astype(BF)
        out_ref[pl.ds(start + i * step, step), :] = done
        half_ref[at, :] = done
        old = noisy_ref[:, pl.ds(start + i * step, step)]
        pos_ref[0:3, at] = old + 0.02 * dot(wcoord_ref[...], done, LANES)

    g_ref[...] = jnp.zeros_like(g_ref)
    chunks = mine // span
    prepare(pos_ref, tab_ref, TABLE_SPAN)

    def sums(i, _):
        s = i // chunks
        at = pl.multiple_of((i % chunks) * span, span)
        u = images(rot_ref, tab_ref, rotor_ref, t_ref, p_ref, s, at, span)
        u = split(u * pos_ref[3:4, pl.ds(at, span)], 2)
        g_ref[...] += dot(u, p_ref[...], LANES)
        return 0

    lax.fori_loop(0, nops * chunks, sums, 0)
    part_ref[:, 0:ROWS] = g_ref[0:32, :] + g_ref[32:64, :]
    quarter = mine // 4
    for i in range(4):
        part_ref[8 * i : 8 * i + 8, ROWS:] = pos_ref[:, i * quarter : (i + 1) * quarter]


def gather_kernel(norm, route_ref, own_ref, other_ref, miller_ref, pay_ref, pos_ref, re_ref, im_ref, f_ref):
    core = lax.axis_index("refl") % 2
    mine = pos_ref.shape[1] // 2
    quarter = mine // 4
    for i in range(4):
        rows = slice(8 * i, 8 * i + 8)
        pos_ref[:, pl.ds(pl.multiple_of(core * mine + i * quarter, quarter), quarter)] = own_ref[rows, ROWS:]
        pos_ref[:, pl.ds(pl.multiple_of((1 - core) * mine + i * quarter, quarter), quarter)] = other_ref[rows, ROWS:]
    grid = split(own_ref[:, 0:ROWS] + other_ref[:, 0:ROWS], 2)
    group = miller_ref.shape[1]
    wide = re_ref.shape[1]
    for c in range(group // wide):
        m = miller_ref[:, c * wide : (c + 1) * wide]
        fill_picks(re_ref, im_ref, m[1:2], m[2:3])
        yr = dot(grid, re_ref[...])
        yi = dot(grid, im_ref[...])
        yr = yr[0:32] + yr[32:64]
        yi = yi[0:32] + yi[32:64]
        uc, us = picks(m[0:1])
        fa = jnp.sum(uc * yr - us * yi, axis=0, keepdims=True) * norm
        fb = jnp.sum(uc * yi + us * yr, axis=0, keepdims=True) * norm
        for b in range(wide // 128):
            row = c * (wide // 128) + b
            f_ref[row : row + 1, :] = fa[:, b * 128 : (b + 1) * 128]
            f_ref[row + 8 : row + 9, :] = fb[:, b * 128 : (b + 1) * 128]

    both = f_ref[...]
    for e in range(pay_ref.shape[0]):
        blk = route_ref[0, e]
        at = pl.multiple_of(lax.shift_right_logical(blk, 1) * 128, 128)
        piece = pos_ref[:, pl.ds(at, 128)]
        odd = jnp.full(piece.shape, blk & 1, jnp.int32) == 1
        pay_ref[e, 0:16, :] = both
        pay_ref[e, 16:24, :] = jnp.where(odd, pltpu.roll(piece, 64, 1), piece)


def gradient_kernel(
    nrefl,
    norm,
    nops,
    span,
    rot_ref,
    shf_ref,
    recv_ref,
    miller_ref,
    obs_ref,
    wt_ref,
    amp_ref,
    grad_ref,
    pos_ref,
    tab_ref,
    rotor_ref,
    t_ref,
    p_ref,
    w_ref,
    re_ref,
    im_ref,
):
    shards = recv_ref.shape[0]
    rotors(rot_ref, shf_ref, rotor_ref)
    total = recv_ref[0, 0:16, :]
    for e in range(1, shards):
        total = total + recv_ref[e, 0:16, :]
    fa, fb = total[0:8], total[8:16]
    amp = jnp.sqrt(fa * fa + fb * fb + 1.0)
    slope = 2.0 * wt_ref[...] * (amp - obs_ref[...]) / (amp * math.sqrt(nrefl))
    amp_ref[...] = amp
    ga, gb = slope * fa, slope * fb
    left = lax.broadcasted_iota(jnp.int32, (8, 128), 1) < 64
    for j in range(shards // 2):
        other = pltpu.roll(recv_ref[2 * j + 1, 16:24, :], 64, 1)
        pos_ref[:, 128 * j : 128 * j + 128] = jnp.where(left, recv_ref[2 * j, 16:24, :], other)

    group = miller_ref.shape[1]
    wide = re_ref.shape[1]
    rows = wide // 128
    for c in range(group // wide):
        m = miller_ref[:, c * wide : (c + 1) * wide]
        fill_picks(re_ref, im_ref, m[1:2], m[2:3])
        uc, us = picks(m[0:1])
        a = jnp.concatenate([ga[c * rows + b : c * rows + b + 1] for b in range(rows)], axis=1)
        b = jnp.concatenate([gb[c * rows + b : c * rows + b + 1] for b in range(rows)], axis=1)
        real = b * uc - a * us
        imag = -(a * uc + b * us)
        mf = m.astype(F32)
        real = jnp.concatenate([mf[k : k + 1] * real for k in range(3)], axis=0).astype(BF)
        imag = jnp.concatenate([mf[k : k + 1] * imag for k in range(3)], axis=0).astype(BF)
        part = dot(real, re_ref[...], LANES) + dot(imag, im_ref[...], LANES)
        w_ref[...] = part if c == 0 else w_ref[...] + part
    coef = w_ref[...].astype(BF)
    local = pos_ref.shape[1]
    grad_ref[...] = jnp.zeros_like(grad_ref)
    chunks = local // span
    factor = 2.0 * math.pi * norm
    prepare(pos_ref, tab_ref, TABLE_SPAN)

    def slopes(i, _):
        s = i // chunks
        at = pl.multiple_of((i % chunks) * span, span)
        u = images(rot_ref, tab_ref, rotor_ref, t_ref, p_ref, s, at, span)
        t = dot(coef, p_ref[...])
        scale = pos_ref[3:4, pl.ds(at, span)] * factor
        g = [jnp.sum(u * t[32 * k : 32 * k + 32], axis=0, keepdims=True) * scale for k in range(3)]
        for c in range(3):
            r = rot_ref[s, 0, c].astype(F32) * g[0]
            r = r + rot_ref[s, 1, c].astype(F32) * g[1]
            r = r + rot_ref[s, 2, c].astype(F32) * g[2]
            grad_ref[c : c + 1, pl.ds(at, span)] += r
        return 0

    lax.fori_loop(0, nops * chunks, slopes, 0)


def body(
    features,
    ln_gain,
    w_qkv,
    w_out,
    w_coord,
    noisy_coords,
    scatter_power,
    route,
    miller,
    rotations,
    shifts,
    observed,
    obs_weight,
):
    shards = lax.axis_size("atom")
    rank = lax.axis_index("atom")
    local = features.shape[0]
    natom = local * shards
    group = miller.shape[1]
    nops = rotations.shape[0]
    nrefl = group * lax.axis_size("refl")
    norm = 1.0 / math.sqrt(nops * natom)
    span = SPAN
    wide = 256
    smem = pl.BlockSpec(memory_space=pltpu.SMEM)
    vmem = pl.BlockSpec(memory_space=pltpu.VMEM)

    core = lax.axis_index("refl") % 2
    mine = local // 2
    ahead = [(g * shards + i, g * shards + i + 1) for g in (0, 2) for i in range(shards - 1)]
    back = [(g * shards + i + 1, g * shards + i) for g in (1, 3) for i in range(shards - 1)]
    edge = lax.dynamic_slice_in_dim(features, (1 - core) * (local - HALO), HALO, 0)
    halo = lax.ppermute(edge, ("refl", "atom"), ahead + back)
    weights = lax.all_gather(w_qkv.transpose(0, 1, 3, 2), "refl")
    params = pltpu.CompilerParams(vmem_limit_bytes=60 * 1024 * 1024)
    swap = [(0, 1), (1, 0), (2, 3), (3, 2)]
    cross = [(0, 2), (2, 0), (1, 3), (3, 1)]
    tables = [
        pltpu.VMEM((3, 80, mine), F32),
        pltpu.VMEM((nops, 2, 96, 128), F32),
        pltpu.VMEM((32, span), F32),
        pltpu.VMEM((ROWS, span), BF),
    ]
    picked = [pltpu.VMEM((ROWS, wide), BF), pltpu.VMEM((ROWS, wide), BF)]
    atoms, half, part = pl.pallas_call(
        functools.partial(attend_kernel, natom, nops, span),
        out_shape=(
            jax.ShapeDtypeStruct((local, 128), BF),
            jax.ShapeDtypeStruct((mine, 128), BF),
            jax.ShapeDtypeStruct((32, ROWS + mine // 4), F32),
        ),
        in_specs=[smem] * 2 + [vmem] * 8,
        out_specs=(vmem,) * 3,
        scratch_shapes=[
            pltpu.VMEM((mine + 2 * HALO, 128), F32),
            pltpu.VMEM((mine + 2 * HALO, 128), F32),
            pltpu.VMEM((mine + 2 * HALO, 128), BF),
            pltpu.VMEM((mine + 2 * HALO, 128), BF),
            pltpu.VMEM((mine + 2 * HALO, 128), BF),
            pltpu.VMEM((8, mine), F32),
            *tables,
            pltpu.VMEM((64, ROWS), F32),
        ],
        compiler_params=params,
        name="attend",
    )(
        rotations,
        shifts,
        features,
        halo,
        weights,
        w_out,
        ln_gain,
        w_coord,
        noisy_coords,
        scatter_power[None, :],
    )
    payload = pl.pallas_call(
        functools.partial(gather_kernel, norm),
        out_shape=jax.ShapeDtypeStruct((shards, 24, 128), F32),
        in_specs=[smem] + [vmem] * 3,
        out_specs=vmem,
        scratch_shapes=[pltpu.VMEM((8, local), F32), *picked, pltpu.VMEM((16, 128), F32)],
        compiler_params=params,
        name="gather",
    )(route, part, lax.ppermute(part, "refl", swap), miller)
    atom_out = lax.dynamic_update_slice_in_dim(
        atoms, lax.ppermute(half, "refl", swap), (1 - core) * mine, 0
    )
    recv = lax.all_to_all(payload, "atom", split_axis=0, concat_axis=0, tiled=True)
    amp, grad = pl.pallas_call(
        functools.partial(gradient_kernel, nrefl, norm, nops, span),
        out_shape=(
            jax.ShapeDtypeStruct((8, 128), F32),
            jax.ShapeDtypeStruct((3, local), F32),
        ),
        in_specs=[smem] * 2 + [vmem] * 4,
        out_specs=(vmem, vmem),
        scratch_shapes=[
            pltpu.VMEM((8, local), F32),
            pltpu.VMEM((3, 80, local), F32),
            *tables[1:],
            pltpu.VMEM((96, ROWS), F32),
            *picked,
        ],
        compiler_params=params,
        name="gradient",
    )(rotations, shifts, recv, miller, observed.reshape(8, 128), obs_weight.reshape(8, 128))
    grad = grad + lax.ppermute(grad, "refl", swap)
    grad = grad + lax.ppermute(grad, "refl", cross)
    share = group // shards
    amplitude = lax.dynamic_slice_in_dim(amp.reshape(group), rank * share, share, 0)
    return (atom_out, amplitude, grad)


def solution(mesh):
    placed = (
        P("atom", None),
        P(),
        P(None, None, None, "refl"),
        P(),
        P(),
        P(None, "atom"),
        P("atom"),
        P("atom", None),
        P(None, "refl"),
        P(),
        P(),
        P("refl"),
        P("refl"),
    )
    return jax.shard_map(
        body,
        mesh=mesh,
        in_specs=placed,
        out_specs=(P("atom", None), P(("refl", "atom")), P(None, "atom")),
        check_vma=False,
    )
```

```python
import functools
import math

import jax
import jax.numpy as jnp
from jax import lax
from jax.experimental import pallas as pl
from jax.experimental.pallas import tpu as pltpu
from jax.sharding import PartitionSpec as P

HEAD = 32
QWIN = 32
KWIN = 128
BORDER = (KWIN - QWIN) // 2
LAYERS = 2
HALO = 128
SPAN = 1024
TABLE_SPAN = 512
TOP = 12
ROWS = 640
BF = jnp.bfloat16
F32 = jnp.float32
LANES = (((1,), (1,)), ((), ()))


def dot(a, b, dims=(((1,), (0,)), ((), ()))):
    return lax.dot_general(a, b, dims, preferred_element_type=F32)


def cos_turns(t):
    t = t - jnp.round(t)
    s = 0.25 - jnp.abs(t)
    z = s * s
    p = 81.6010046 + z * (39.5368083 * z - 76.5497956)
    return s * (6.28318516 + z * (z * p - 41.341655))


COSINES = TOP + 1
ORDER = list(range(COSINES)) + list(range(17, 17 + TOP))


def part_rows(i):
    sine = i >= TOP
    freq = jnp.where(i >= 16, i - 15, jnp.where(sine, i - 3, i))
    return freq.astype(F32), sine


def prepare(pos_ref, tab_ref, span):
    row = lax.broadcasted_iota(jnp.int32, (8, span), 0)
    bits = [(row & (1 << b)) != 0 for b in range(3)]
    low = row < 4

    def fill(i, _):
        at = pl.multiple_of(i * span, span)
        x = pos_ref[:, pl.ds(at, span)]
        cos_x, sin_x = cos_turns(x), cos_turns(x - 0.25)
        for k in range(3):
            c1 = jnp.broadcast_to(cos_x[k : k + 1], row.shape)
            s1 = jnp.broadcast_to(sin_x[k : k + 1], row.shape)
            c2, s2 = 1.0 - 2.0 * (s1 * s1), 2.0 * (s1 * c1)
            c4, s4 = 1.0 - 2.0 * (s2 * s2), 2.0 * (s2 * c2)
            c8, s8 = 1.0 - 2.0 * (s4 * s4), 2.0 * (s4 * c4)
            c, s = jnp.where(bits[0], c1, 1.0), jnp.where(bits[0], s1, 0.0)
            for bit, cm, sm in ((bits[1], c2, s2), (bits[2], c4, s4)):
                c, s = jnp.where(bit, c * cm - s * sm, c), jnp.where(bit, s * cm + c * sm, s)
            cb, sb = c * c8 - s * s8, s * c8 + c * s8
            cn, sn = c * c1 - s * s1, s * c1 + c * s1
            ct, st = cn * c8 - sn * s8, sn * c8 + cn * s8
            mid = jnp.where(low, cb, pltpu.roll(st, 4, 0))
            mid_other = jnp.where(low, sb, pltpu.roll(ct, 4, 0))
            for r, part in enumerate((c, cb, s, sb, c, mid, sn, s, mid_other, cn)):
                tab_ref[k, 8 * r : 8 * r + 8, pl.ds(at, span)] = part
        return 0

    lax.fori_loop(0, pos_ref.shape[1] // span, fill, 0)


def rotors(rot_ref, shf_ref, rotor_ref):
    lane = lax.broadcasted_iota(jnp.int32, (1, 128), 1)
    turn = jnp.zeros((1, 128), F32)
    sign = jnp.ones((1, 128), F32)
    nops = rotor_ref.shape[0]
    for s in range(nops):
        for k in range(3):
            here = lane == 3 * s + k
            whole = rot_ref[k, s, 0] + rot_ref[k, s, 1] + rot_ref[k, s, 2]
            turn = jnp.where(here, shf_ref[s, k], turn)
            sign = jnp.where(here, whole.astype(F32), sign)
    i = lax.broadcasted_iota(jnp.int32, (32, 1), 0)
    tables = [((i % 16).astype(F32), i >= 16)] * 2
    tables.append(part_rows(lax.broadcasted_iota(jnp.int32, (24, 1), 0)))
    for k, (freq, sine) in enumerate(tables):
        angle = freq * turn
        same = cos_turns(angle) * jnp.where(sine, sign, 1.0)
        other = cos_turns(angle - 0.25) * jnp.where(sine, 1.0, -sign)
        size = freq.shape[0]
        for s in range(nops):
            j = 3 * s + k
            spread = (size, 128)
            rotor_ref[s, 0, 32 * k : 32 * k + size, :] = jnp.broadcast_to(same[:, j : j + 1], spread)
            rotor_ref[s, 1, 32 * k : 32 * k + size, :] = jnp.broadcast_to(other[:, j : j + 1], spread)
    freq = jnp.full((8, 1), float(TOP), F32)
    same, other = cos_turns(freq * turn), cos_turns(freq * turn - 0.25) * -sign
    for s in range(nops):
        j = 3 * s + 2
        rotor_ref[s, 0, 88:96, :] = jnp.broadcast_to(same[:, j : j + 1], (8, 128))
        rotor_ref[s, 1, 88:96, :] = jnp.broadcast_to(other[:, j : j + 1], (8, 128))


def images(rot_ref, tab_ref, rotor_ref, v_ref, p_ref, s, at, span):
    def table(k, r, size):
        axis = jnp.abs(rot_ref[k, s, 1]) + 2 * jnp.abs(rot_ref[k, s, 2])
        return tab_ref[axis, r : r + size, pl.ds(at, span)]

    def factor(kind, r, size):
        return jnp.concatenate([rotor_ref[s, kind, r : r + size, :]] * (span // 128), axis=1)

    def both(k):
        c, n = table(k, 0, 16), table(k, 16, 16)
        cos = factor(0, 32 * k, 16) * c + factor(1, 32 * k, 16) * n
        sin = factor(0, 32 * k + 16, 16) * n + factor(1, 32 * k + 16, 16) * c
        return jnp.concatenate([cos, sin], axis=0)

    v = both(1)
    v_ref[...] = v
    w = factor(0, 64, 24) * table(2, 32, 24) + factor(1, 64, 24) * table(2, 56, 24)
    c12 = table(2, 8, 8)[4:5]
    s12 = table(2, 24, 8)[4:5]
    last = factor(0, 88, 8)[0:1] * c12 + factor(1, 88, 8)[0:1] * s12

    def row(j):
        return v_ref[ORDER[j] : ORDER[j] + 1, :]

    def spread(j):
        return jnp.broadcast_to(row(j), (24, span))

    w2 = jnp.concatenate([w, w], axis=0).astype(BF)
    for j in range(TOP):
        pair = jnp.concatenate([spread(2 * j), spread(2 * j + 1)], axis=0).astype(BF)
        p_ref[48 * j : 48 * j + 48, :] = pair * w2
    pad = jnp.zeros((8, span), F32)
    p_ref[576:640, :] = jnp.concatenate([row(24) * w, v * last, pad], axis=0).astype(BF)
    return both(0)


def picks(m):
    i = lax.broadcasted_iota(jnp.int32, (32, m.shape[1]), 0)
    size = jnp.abs(m)
    sign = jnp.clip(m, -1, 1).astype(F32)
    return (
        jnp.where(i == size, 1.0, 0.0).astype(F32),
        jnp.where(i == size + 16, sign, 0.0).astype(F32),
    )


def fill_picks(re_ref, im_ref, k, l):
    ck, sk = picks(k)
    i = lax.broadcasted_iota(jnp.int32, (24, l.shape[1]), 0)
    size = jnp.abs(l)
    sign = jnp.clip(l, -1, 1).astype(F32)
    cl = jnp.where(i == jnp.where(size < TOP, size, -1), 1.0, 0.0).astype(F32)
    sl = jnp.where(i == jnp.where(size >= 9, size + 3, size + 15), sign, 0.0).astype(F32)
    top = jnp.where(size == TOP, 1.0, 0.0).astype(F32)

    def real(j):
        r = ORDER[j]
        return ck[r : r + 1] * cl if r < 16 else -sk[r : r + 1] * sl

    def imag(j):
        r = ORDER[j]
        return ck[r : r + 1] * sl if r < 16 else sk[r : r + 1] * cl

    pad = jnp.zeros((8, k.shape[1]), F32)
    for ref, own, tail in ((re_ref, real, ck * top), (im_ref, imag, sk * top)):
        for j in range(TOP):
            pair = jnp.concatenate([own(2 * j), own(2 * j + 1)], axis=0)
            ref[48 * j : 48 * j + 48, :] = pair.astype(BF)
        ref[576:640, :] = jnp.concatenate([own(24), tail, pad], axis=0).astype(BF)


def split(a, count):
    parts = []
    for _ in range(count):
        hi = a.astype(BF)
        parts.append(hi)
        a = a - hi.astype(F32)
    return jnp.concatenate(parts, axis=0)


def attend_kernel(
    natom,
    nops,
    span,
    rot_ref,
    shf_ref,
    feat_ref,
    halo_ref,
    wqkv_ref,
    wout_ref,
    gain_ref,
    wcoord_ref,
    noisy_ref,
    power_ref,
    out_ref,
    half_ref,
    part_ref,
    x_ref,
    x1_ref,
    q_ref,
    k_ref,
    v_ref,
    pos_ref,
    tab_ref,
    rotor_ref,
    t_ref,
    p0_ref,
    p1_ref,
    g_ref,
):
    p_refs = (p0_ref, p1_ref)
    mine = half_ref.shape[0]
    core = lax.axis_index("refl") % 2
    start = pl.multiple_of(core * mine, mine)
    rotors(rot_ref, shf_ref, rotor_ref)
    first_half = jnp.full((HALO, 128), core, jnp.int32) == 0
    halo = halo_ref[...].astype(F32)
    left = feat_ref[mine - HALO : mine, :].astype(F32)
    right = feat_ref[mine : mine + HALO, :].astype(F32)
    x_ref[0:HALO, :] = jnp.where(first_half, halo, left)
    x_ref[HALO : HALO + mine, :] = feat_ref[pl.ds(start, mine), :].astype(F32)
    x_ref[HALO + mine :, :] = jnp.where(first_half, right, halo)
    origin = lax.axis_index("atom") * feat_ref.shape[0] + start - HALO
    head_of = lax.broadcasted_iota(jnp.int32, (QWIN, 128), 1) // HEAD
    lane = lax.broadcasted_iota(jnp.int32, (1, KWIN), 1)
    scale = HEAD**-0.5 * math.log2(math.e)

    for layer in range(LAYERS):
        edge = 64 * layer
        size = x_ref.shape[0]
        part = min(size // 2, 640)
        from_ref, dest_ref = (x_ref, x1_ref) if layer == 0 else (x1_ref, x_ref)
        weights = jnp.concatenate(
            [wqkv_ref[g, layer, j] for j in range(3) for g in range(4)], axis=0
        )
        gain = gain_ref[layer : layer + 1, :]

        def project(i, _):
            r = pl.multiple_of(jnp.minimum(edge + i * part, size - edge - part), 64)
            xc = from_ref[pl.ds(r, part), :]
            cent = xc - jnp.mean(xc, axis=1, keepdims=True)
            var = jnp.mean(cent * cent, axis=1, keepdims=True)
            normed = (cent * lax.rsqrt(var + 1e-05) * gain).astype(BF)
            proj = dot(normed, weights, LANES).astype(BF)
            q_ref[pl.ds(r, part), :] = proj[:, 0:128]
            k_ref[pl.ds(r, part), :] = proj[:, 128:256]
            v_ref[pl.ds(r, part), :] = proj[:, 256:384]
            return 0

        lax.fori_loop(0, -(-(size - 2 * edge) // part), project, 0)
        w_out = wout_ref[layer]
        first = 64 * (layer + 1)
        rows = mine + 128 * (1 - layer)
        block = 64 * -(-rows // 128)
        ones = jnp.ones((KWIN, 128), BF)

        def attend(i, _):
            base = pl.multiple_of(jnp.minimum(first + i * block, first + rows - block), 64)
            scores = []
            for win in range(block // QWIN):
                r = base + win * QWIN
                qw = q_ref[pl.ds(pl.multiple_of(r, 32), QWIN), :]
                at = pl.multiple_of(r - BORDER, 16)
                kw = k_ref[pl.ds(at, KWIN), :]
                qm = jnp.concatenate(
                    [jnp.where(head_of == h, qw, jnp.zeros_like(qw)) for h in range(4)], axis=0
                )
                s = dot(qm, kw, LANES)
                place = lane + (origin + at)
                scores.append(jnp.where((place >= 0) & (place < natom), s, -1e30))
            tops = [jnp.max(s, axis=1, keepdims=True) for s in scores]
            heads = []
            for win in range(block // QWIN):
                at = pl.multiple_of(base + win * QWIN - BORDER, 16)
                vw = v_ref[pl.ds(at, KWIN), :]
                e = jnp.exp2((scores[win] - tops[win]) * scale).astype(BF)
                o = dot(e, jnp.concatenate([vw, ones], axis=1))
                o = o[:, 0:128] / o[:, 128:256]
                own = jnp.zeros((QWIN, 128), F32)
                for h in range(4):
                    own = jnp.where(head_of == h, o[QWIN * h : QWIN * h + QWIN], own)
                heads.append(own.astype(BF))
            y = dot(jnp.concatenate(heads, axis=0), w_out)
            dest_ref[pl.ds(base, block), :] = from_ref[pl.ds(base, block), :] + y
            return 0

        lax.fori_loop(0, -(-rows // block), attend, 0)

    pos_ref[...] = jnp.zeros_like(pos_ref)
    pos_ref[3:4, :] = power_ref[:, pl.ds(start, mine)]
    step = 256
    for i in range(mine // step):
        at = slice(i * step, (i + 1) * step)
        done = x_ref[HALO + i * step : HALO + (i + 1) * step, :].astype(BF)
        out_ref[pl.ds(start + i * step, step), :] = done
        half_ref[at, :] = done
        old = noisy_ref[:, pl.ds(start + i * step, step)]
        pos_ref[0:3, at] = old + 0.02 * dot(wcoord_ref[...], done, LANES)

    g_ref[...] = jnp.zeros_like(g_ref)
    chunks = mine // span
    prepare(pos_ref, tab_ref, TABLE_SPAN)

    def sums(i, _):
        at = pl.multiple_of(i * span, span)
        power = pos_ref[3:4, pl.ds(at, span)]
        total = g_ref[...]
        for s in range(nops):
            p_ref = p_refs[s % 2]
            u = images(rot_ref, tab_ref, rotor_ref, t_ref.at[s % 2], p_ref, s, at, span)
            total = total + dot(split(u * power, 2), p_ref[...], LANES)
        g_ref[...] = total
        return 0

    lax.fori_loop(0, chunks, sums, 0)
    part_ref[:, 0:ROWS] = g_ref[0:32, :] + g_ref[32:64, :]
    quarter = mine // 4
    for i in range(4):
        part_ref[8 * i : 8 * i + 8, ROWS:] = pos_ref[:, i * quarter : (i + 1) * quarter]


def gather_kernel(norm, route_ref, own_ref, other_ref, miller_ref, pay_ref, pos_ref, re_ref, im_ref, f_ref):
    core = lax.axis_index("refl") % 2
    mine = pos_ref.shape[1] // 2
    quarter = mine // 4
    for i in range(4):
        rows = slice(8 * i, 8 * i + 8)
        pos_ref[:, pl.ds(pl.multiple_of(core * mine + i * quarter, quarter), quarter)] = own_ref[rows, ROWS:]
        pos_ref[:, pl.ds(pl.multiple_of((1 - core) * mine + i * quarter, quarter), quarter)] = other_ref[rows, ROWS:]
    grid = split(own_ref[:, 0:ROWS] + other_ref[:, 0:ROWS], 2)
    group = miller_ref.shape[1]
    wide = re_ref.shape[1]
    for c in range(group // wide):
        m = miller_ref[:, c * wide : (c + 1) * wide]
        fill_picks(re_ref, im_ref, m[1:2], m[2:3])
        yr = dot(grid, re_ref[...])
        yi = dot(grid, im_ref[...])
        yr = yr[0:32] + yr[32:64]
        yi = yi[0:32] + yi[32:64]
        uc, us = picks(m[0:1])
        fa = jnp.sum(uc * yr - us * yi, axis=0, keepdims=True) * norm
        fb = jnp.sum(uc * yi + us * yr, axis=0, keepdims=True) * norm
        for b in range(wide // 128):
            row = c * (wide // 128) + b
            f_ref[row : row + 1, :] = fa[:, b * 128 : (b + 1) * 128]
            f_ref[row + 8 : row + 9, :] = fb[:, b * 128 : (b + 1) * 128]

    both = f_ref[...]
    for e in range(pay_ref.shape[0]):
        blk = route_ref[0, e]
        at = pl.multiple_of(lax.shift_right_logical(blk, 1) * 128, 128)
        piece = pos_ref[:, pl.ds(at, 128)]
        odd = jnp.full(piece.shape, blk & 1, jnp.int32) == 1
        pay_ref[e, 0:16, :] = both
        pay_ref[e, 16:24, :] = jnp.where(odd, pltpu.roll(piece, 64, 1), piece)


def gradient_kernel(
    nrefl,
    norm,
    nops,
    span,
    rot_ref,
    shf_ref,
    recv_ref,
    miller_ref,
    obs_ref,
    wt_ref,
    amp_ref,
    grad_ref,
    pos_ref,
    tab_ref,
    rotor_ref,
    t_ref,
    p0_ref,
    p1_ref,
    w_ref,
    re_ref,
    im_ref,
):
    p_refs = (p0_ref, p1_ref)
    shards = recv_ref.shape[0]
    rotors(rot_ref, shf_ref, rotor_ref)
    total = recv_ref[0, 0:16, :]
    for e in range(1, shards):
        total = total + recv_ref[e, 0:16, :]
    fa, fb = total[0:8], total[8:16]
    amp = jnp.sqrt(fa * fa + fb * fb + 1.0)
    slope = 2.0 * wt_ref[...] * (amp - obs_ref[...]) / (amp * math.sqrt(nrefl))
    amp_ref[...] = amp
    ga, gb = slope * fa, slope * fb
    left = lax.broadcasted_iota(jnp.int32, (8, 128), 1) < 64
    for j in range(shards // 2):
        other = pltpu.roll(recv_ref[2 * j + 1, 16:24, :], 64, 1)
        pos_ref[:, 128 * j : 128 * j + 128] = jnp.where(left, recv_ref[2 * j, 16:24, :], other)

    group = miller_ref.shape[1]
    wide = re_ref.shape[1]
    rows = wide // 128
    for c in range(group // wide):
        m = miller_ref[:, c * wide : (c + 1) * wide]
        fill_picks(re_ref, im_ref, m[1:2], m[2:3])
        uc, us = picks(m[0:1])
        a = jnp.concatenate([ga[c * rows + b : c * rows + b + 1] for b in range(rows)], axis=1)
        b = jnp.concatenate([gb[c * rows + b : c * rows + b + 1] for b in range(rows)], axis=1)
        real = b * uc - a * us
        imag = -(a * uc + b * us)
        mf = m.astype(F32)
        real = jnp.concatenate([mf[k : k + 1] * real for k in range(3)], axis=0).astype(BF)
        imag = jnp.concatenate([mf[k : k + 1] * imag for k in range(3)], axis=0).astype(BF)
        part = dot(real, re_ref[...], LANES) + dot(imag, im_ref[...], LANES)
        w_ref[...] = part if c == 0 else w_ref[...] + part
    coef = w_ref[...].astype(BF)
    local = pos_ref.shape[1]
    chunks = local // span
    factor = 2.0 * math.pi * norm
    prepare(pos_ref, tab_ref, TABLE_SPAN)

    def slopes(i, _):
        at = pl.multiple_of(i * span, span)
        scale = pos_ref[3:4, pl.ds(at, span)] * factor
        total = [jnp.zeros((1, span), F32)] * 3
        for s in range(nops):
            p_ref = p_refs[s % 2]
            u = images(rot_ref, tab_ref, rotor_ref, t_ref.at[s % 2], p_ref, s, at, span)
            t = dot(coef, p_ref[...])
            g = [jnp.sum(u * t[32 * k : 32 * k + 32], axis=0, keepdims=True) for k in range(3)]
            for c in range(3):
                for k in range(3):
                    total[c] = total[c] + rot_ref[k, s, c].astype(F32) * g[k]
        for c in range(3):
            grad_ref[c : c + 1, pl.ds(at, span)] = total[c] * scale
        return 0

    lax.fori_loop(0, chunks, slopes, 0)


def body(
    features,
    ln_gain,
    w_qkv,
    w_out,
    w_coord,
    noisy_coords,
    scatter_power,
    route,
    miller,
    rotations,
    shifts,
    observed,
    obs_weight,
):
    shards = lax.axis_size("atom")
    rank = lax.axis_index("atom")
    local = features.shape[0]
    natom = local * shards
    group = miller.shape[1]
    nops = rotations.shape[0]
    nrefl = group * lax.axis_size("refl")
    norm = 1.0 / math.sqrt(nops * natom)
    span = SPAN
    wide = 256
    smem = pl.BlockSpec(memory_space=pltpu.SMEM)
    vmem = pl.BlockSpec(memory_space=pltpu.VMEM)

    core = lax.axis_index("refl") % 2
    mine = local // 2
    ahead = [(g * shards + i, g * shards + i + 1) for g in (0, 2) for i in range(shards - 1)]
    back = [(g * shards + i + 1, g * shards + i) for g in (1, 3) for i in range(shards - 1)]
    edge = lax.dynamic_slice_in_dim(features, (1 - core) * (local - HALO), HALO, 0)
    halo = lax.ppermute(edge, ("refl", "atom"), ahead + back)
    weights = lax.all_gather(w_qkv.transpose(0, 1, 3, 2), "refl")
    turns = rotations.transpose(1, 0, 2)
    params = pltpu.CompilerParams(vmem_limit_bytes=24 * 1024 * 1024)
    swap = [(0, 1), (1, 0), (2, 3), (3, 2)]
    cross = [(0, 2), (2, 0), (1, 3), (3, 1)]
    tables = [
        pltpu.VMEM((3, 80, mine), F32),
        pltpu.VMEM((nops, 2, 96, 128), F32),
        pltpu.VMEM((2, 32, span), F32),
        pltpu.VMEM((ROWS, span), BF),
        pltpu.VMEM((ROWS, span), BF),
    ]
    picked = [pltpu.VMEM((ROWS, wide), BF), pltpu.VMEM((ROWS, wide), BF)]
    atoms, half, part = pl.pallas_call(
        functools.partial(attend_kernel, natom, nops, span),
        out_shape=(
            jax.ShapeDtypeStruct((local, 128), BF),
            jax.ShapeDtypeStruct((mine, 128), BF),
            jax.ShapeDtypeStruct((32, ROWS + mine // 4), F32),
        ),
        in_specs=[smem] * 2 + [vmem] * 8,
        out_specs=(vmem,) * 3,
        scratch_shapes=[
            pltpu.VMEM((mine + 2 * HALO, 128), F32),
            pltpu.VMEM((mine + 2 * HALO, 128), F32),
            pltpu.VMEM((mine + 2 * HALO, 128), BF),
            pltpu.VMEM((mine + 2 * HALO, 128), BF),
            pltpu.VMEM((mine + 2 * HALO, 128), BF),
            pltpu.VMEM((8, mine), F32),
            *tables,
            pltpu.VMEM((64, ROWS), F32),
        ],
        compiler_params=params,
        name="attend",
    )(
        turns,
        shifts,
        features,
        halo,
        weights,
        w_out,
        ln_gain,
        w_coord,
        noisy_coords,
        scatter_power[None, :],
    )
    payload = pl.pallas_call(
        functools.partial(gather_kernel, norm),
        out_shape=jax.ShapeDtypeStruct((shards, 24, 128), F32),
        in_specs=[smem] + [vmem] * 3,
        out_specs=vmem,
        scratch_shapes=[pltpu.VMEM((8, local), F32), *picked, pltpu.VMEM((16, 128), F32)],
        compiler_params=params,
        name="gather",
    )(route, part, lax.ppermute(part, "refl", swap), miller)
    atom_out = lax.dynamic_update_slice_in_dim(
        atoms, lax.ppermute(half, "refl", swap), (1 - core) * mine, 0
    )
    recv = lax.all_to_all(payload, "atom", split_axis=0, concat_axis=0, tiled=True)
    amp, grad = pl.pallas_call(
        functools.partial(gradient_kernel, nrefl, norm, nops, span),
        out_shape=(
            jax.ShapeDtypeStruct((8, 128), F32),
            jax.ShapeDtypeStruct((3, local), F32),
        ),
        in_specs=[smem] * 2 + [vmem] * 4,
        out_specs=(vmem, vmem),
        scratch_shapes=[
            pltpu.VMEM((8, local), F32),
            pltpu.VMEM((3, 80, local), F32),
            *tables[1:],
            pltpu.VMEM((96, ROWS), F32),
            *picked,
        ],
        compiler_params=params,
        name="gradient",
    )(turns, shifts, recv, miller, observed.reshape(8, 128), obs_weight.reshape(8, 128))
    grad = grad + lax.ppermute(grad, "refl", swap)
    grad = grad + lax.ppermute(grad, "refl", cross)
    share = group // shards
    amplitude = lax.dynamic_slice_in_dim(amp.reshape(group), rank * share, share, 0)
    return (atom_out, amplitude, grad)


def solution(mesh):
    placed = (
        P("atom", None),
        P(),
        P(None, None, None, "refl"),
        P(),
        P(),
        P(None, "atom"),
        P("atom"),
        P("atom", None),
        P(None, "refl"),
        P(),
        P(),
        P("refl"),
        P("refl"),
    )
    return jax.shard_map(
        body,
        mesh=mesh,
        in_specs=placed,
        out_specs=(P("atom", None), P(("refl", "atom")), P(None, "atom")),
        check_vma=False,
    )
```
